512 devices in a mesh: rows: 512 (over y, x, z, core).
Axes of the slice: x: 4, y: 8, z: 8, core: 2. Of those that a mesh axis runs over, the one named last changes fastest.
Arguments:
- rhs: float32 [131072, 512], P('rows'), may hold values from -6 to 6
- v_basis0: float32 [131072, 256], P('rows'), may hold values from -0.0234375 to 0.0234375
- w_basis0: float32 [131072, 256], P('rows'), may hold values from -0.375 to 0.375
- cap_inv0: float32 [512, 512], P('rows'), may hold values from -0.25 to 0.25
- v_basis1: float32 [131072, 256], P('rows'), may hold values from -0.03125 to 0.03125
- w_basis1: float32 [131072, 256], P('rows'), may hold values from -0.375 to 0.375
- cap_inv1: float32 [1024, 512], P('rows'), may hold values from -0.25 to 0.25
- v_basis2: float32 [131072, 256], P('rows'), may hold values from -0.046875 to 0.046875
- w_basis2: float32 [131072, 256], P('rows'), may hold values from -0.375 to 0.375
- cap_inv2: float32 [2048, 512], P('rows'), may hold values from -0.25 to 0.25
Outputs:
- solved: float32 [131072, 512], P('rows')
The draws below stay inside these ranges and needn't reach their ends.
All inputs are finite; a program needn't handle non-finite values.
Results may differ from the reference program's by a relative error of at most 0.00014.
Values sent between devices are 32-bit elements; how exact they have to be, the bound alone decides.
A program may use at most 64 MiB of HBM per device.

```python
import jax
import jax.numpy as jnp
from jax import lax

K = 256
NRHS = 512
NTOT = 131072


def steps_of(rng, extent, pieces, low, top_value):
    factor_of, own = 1.0, jax.random.fold_in(rng, 6)
    for position, parts in pieces:
        draws = jnp.exp(jax.random.uniform(jax.random.fold_in(own, position), (parts,), jnp.float32, low / len(pieces), top_value / len(pieces)))
        factor_of = factor_of * jnp.repeat(draws, extent[position] // parts).reshape([-1 if axis == position else 1 for axis in range(len(extent))])
    return factor_of


def bell_draw(key, shape, scale, most, split=(), kind=jnp.bfloat16):
    values = scale * jax.random.normal(key, shape, jnp.float32)
    if split:
        values = values * steps_of(key, shape, split, -0.22, 0.18)
    return jnp.clip(values, -most, most).astype(kind)


def setup_inputs(seed: int = 0) -> dict:
    arg_keys = jax.random.split(jax.random.key(seed), 11)
    return {
        "rhs": bell_draw(arg_keys[0], (NTOT, NRHS), 1.0, 6.0, ((0, 512),), jnp.float32),
        "v_basis0": bell_draw(arg_keys[1], (NTOT, K), (NTOT // 2) ** -0.5, 0.0234375, ((0, 512),), jnp.float32),
        "w_basis0": bell_draw(arg_keys[2], (NTOT, K), K ** -0.5, 0.375, ((0, 512),), jnp.float32),
        "cap_inv0": bell_draw(arg_keys[3], (2 * K, 2 * K), (2 * K) ** -0.5, 0.25, ((0, 512),), jnp.float32),
        "v_basis1": bell_draw(arg_keys[4], (NTOT, K), (NTOT // 4) ** -0.5, 0.03125, ((0, 512),), jnp.float32),
        "w_basis1": bell_draw(arg_keys[5], (NTOT, K), K ** -0.5, 0.375, ((0, 512),), jnp.float32),
        "cap_inv1": bell_draw(arg_keys[6], (4 * K, 2 * K), (2 * K) ** -0.5, 0.25, ((0, 512),), jnp.float32),
        "v_basis2": bell_draw(arg_keys[7], (NTOT, K), (NTOT // 8) ** -0.5, 0.046875, ((0, 512),), jnp.float32),
        "w_basis2": bell_draw(arg_keys[8], (NTOT, K), K ** -0.5, 0.375, ((0, 512),), jnp.float32),
        "cap_inv2": bell_draw(arg_keys[9], (8 * K, 2 * K), (2 * K) ** -0.5, 0.25, ((0, 512),), jnp.float32),
    }


def apply_level(state, v_basis, w_basis, cap_inv, level):
    children = 2 ** (level + 1)
    rows_child = state.shape[0] // children
    x_blocks = state.reshape(children, rows_child, state.shape[1])
    v_blocks = v_basis.reshape(children, rows_child, v_basis.shape[1])
    w_blocks = w_basis.reshape(children, rows_child, w_basis.shape[1])
    proj = jnp.einsum("csk,csn->ckn", v_blocks, x_blocks, precision=lax.Precision.HIGHEST)
    pairs = proj.reshape(children // 2, 2, proj.shape[1], proj.shape[2])
    stacked = jnp.concatenate([pairs[:, 1], pairs[:, 0]], axis=1)
    cap_blocks = cap_inv.reshape(children // 2, 2, proj.shape[1], cap_inv.shape[1])
    coef = jnp.einsum("mikj,mjn->mikn", cap_blocks, stacked, precision=lax.Precision.HIGHEST)
    coef = coef.reshape(children, proj.shape[1], proj.shape[2])
    update = jnp.einsum("csk,ckn->csn", w_blocks, coef, precision=lax.Precision.HIGHEST)
    return (x_blocks - update).reshape(state.shape)


def reference(rhs, v_basis0, w_basis0, cap_inv0, v_basis1, w_basis1, cap_inv1, v_basis2, w_basis2, cap_inv2):
    state = apply_level(rhs, v_basis2, w_basis2, cap_inv2, 2)
    state = apply_level(state, v_basis1, w_basis1, cap_inv1, 1)
    state = apply_level(state, v_basis0, w_basis0, cap_inv0, 0)
    return state
```

```python
import jax
import jax.numpy as jnp
from jax import lax
from jax.experimental import pallas as pl
from jax.experimental.pallas import tpu as pltpu
from jax.sharding import PartitionSpec as P

MESH = pl.DeviceIdType.MESH
F32 = jnp.float32
NX, NZ, NC, NY = 4, 8, 2, 8
K, N, R = 256, 512, 8


def dot(a, b, dims=((1,), (0,))):
    return lax.dot_general(
        a, b, (dims, ((), ())), precision=lax.Precision.HIGHEST, preferred_element_type=F32
    )


def pick(rows_of, source_rows):
    row = lax.broadcasted_iota(jnp.int32, (K, source_rows), 0)
    column = lax.broadcasted_iota(jnp.int32, (K, source_rows), 1)
    return (column == rows_of(row)).astype(F32)


def slot_row(member):
    return 8 * ((member % 2) * 32 + member // 2)


def kernel(
    x_ref, v0_ref, w0_ref, cap0_ref, v1_ref, w1_ref, cap1_ref, v2_ref, w2_ref, cap2_ref,
    out_ref,
    gram, q2, q10, gram_c, q2_c, q10_c, gram_x, q2_x, q10_x, gram_z, q2_z, q10_z,
    gram_all, cap_all, c2_all, c1_all, c0_all,
    cap1_y, cap0_y, q2_y, q1_y, q0_y,
    send_sem, recv_sem,
):
    me = lax.axis_index("rows")
    y, x, z, c = me // 64, (me // 16) % 4, (me // 2) % 8, me % 2
    other = 1 - c
    half = pl.multiple_of(c * 256, 256)
    other_half = pl.multiple_of(other * 256, 256)
    block = pl.multiple_of(c * 256 + x * 64, 64)
    own = pl.multiple_of(c * 256 + x * 64 + z * 8, 8)

    def at(yy, xx, zz, cc):
        return ((yy * 4 + xx) * 8 + zz) * 2 + cc

    def flip(k):
        b0, b1, b2 = y % 2, (y // 2) % 2, y // 4
        b0 = 1 - b0 if k & 1 else b0
        b1 = 1 - b1 if k & 2 else b1
        b2 = 1 - b2 if k & 4 else b2
        return b2 * 4 + b1 * 2 + b0

    core = at(y, x, z, other)
    along_x = [((x + k) % 4, at(y, (x + k) % 4, z, c)) for k in range(1, 4)]
    along_z = [((z + k) % 8, at(y, x, (z + k) % 8, c)) for k in range(1, 8)]
    along_y = [at(flip(k), x, z, c) for k in range(1, 8)]

    barrier = pltpu.get_barrier_semaphore()
    everyone = [core] + [d for _, d in along_x] + [d for _, d in along_z] + along_y
    for device in everyone:
        pl.semaphore_signal(barrier, inc=1, device_id=(device,), device_id_type=MESH)

    used = [0]
    started = []

    def send(source, target, device):
        index = used[0]
        used[0] += 1
        copy = pltpu.make_async_remote_copy(
            src_ref=source,
            dst_ref=target,
            send_sem=send_sem.at[index],
            recv_sem=recv_sem.at[index],
            device_id=(device,),
            device_id_type=MESH,
        )
        copy.start()
        started.append(copy)
        return copy

    def arrived(copies):
        for copy in copies:
            copy.wait_recv()

    def core_step(buffer, landing):
        return [send(buffer.at[pl.ds(other_half, 256)], landing, core)]

    def core_sum(buffer, landing, copies):
        arrived(copies)
        buffer[pl.ds(half, 256), :] += landing[...]

    def x_step(buffer, landing):
        return [
            send(
                buffer.at[pl.ds(pl.multiple_of(c * 256 + xx * 64, 64), 64)], landing.at[k], device
            )
            for k, (xx, device) in enumerate(along_x)
        ]

    def x_sum(buffer, landing, copies):
        arrived(copies)
        buffer[pl.ds(block, 64), :] += landing[0] + landing[1] + landing[2]

    def z_step(buffer, landing):
        return [
            send(
                buffer.at[pl.ds(pl.multiple_of(c * 256 + x * 64 + zz * 8, 8), 8)],
                landing.at[k],
                device,
            )
            for k, (zz, device) in enumerate(along_z)
        ]

    def z_sum(buffer, landing, copies):
        arrived(copies)
        total = buffer[pl.ds(own, 8), :]
        for k in range(7):
            total = total + landing[k]
        return total

    def gather_z(full):
        part = full.at[pl.ds(own, 8)]
        return [send(part, part, device) for _, device in along_z]

    def gather_x(full, copies):
        arrived(copies)
        part = full.at[pl.ds(block, 64)]
        return [send(part, part, device) for _, device in along_x]

    def gather_core(full, copies):
        arrived(copies)
        part = full.at[pl.ds(half, 256)]
        return [send(part, part, core)]

    w2_t, w1_t = w2_ref[...].T, w1_ref[...].T
    gram[0:256, 0:256] = dot(w2_t, v1_ref[...])
    gram[256:512, 0:256] = dot(w2_t, v0_ref[...])
    cross = dot(w1_t, v0_ref[...])
    gram[0:256, 256:384] = cross[:, 0:128]
    gram[256:512, 256:384] = cross[:, 128:256]

    cap1_y[y % 2] = cap1_ref[...]
    cap0_y[y % 4] = cap0_ref[...]

    pl.semaphore_wait(barrier, len(everyone))
    gram_copies = core_step(gram, gram_c)

    x_t = x_ref[...].T
    q2[...] = dot(x_t, v2_ref[...])
    q2_copies = core_step(q2, q2_c)
    cap_copies = [send(cap1_ref, cap1_y.at[y % 2], along_y[0])]
    cap_copies += [send(cap0_ref, cap0_y.at[y % 4], along_y[k]) for k in range(3)]
    core_sum(gram, gram_c, gram_copies)
    gram_copies = x_step(gram, gram_x)
    core_sum(q2, q2_c, q2_copies)
    q2_copies = x_step(q2, q2_x)

    q10[:, 0:256] = dot(x_t, v1_ref[...])
    q10[:, 256:512] = dot(x_t, v0_ref[...])
    q10_copies = core_step(q10, q10_c)

    arrived(cap_copies)
    rows = pl.ds(own, 8)
    lower = jnp.concatenate([cap2_ref[...], cap1_y[0], cap1_y[1]], axis=0)
    upper = jnp.concatenate(
        [cap0_y[t][:, 0:256] for t in range(4)] + [cap0_y[t][:, 256:512] for t in range(4)], axis=0
    )
    cap_all[rows, 0:512] = lower
    cap_all[rows, 512:768] = upper
    cap_copies = gather_z(cap_all)

    core_sum(q10, q10_c, q10_copies)
    x_sum(gram, gram_x, gram_copies)
    gram_copies = z_step(gram, gram_z)
    x_sum(q2, q2_x, q2_copies)
    q2_copies = z_step(q2, q2_z)
    q10_copies = x_step(q10, q10_x)
    cap_copies = gather_x(cap_all, cap_copies)

    gram_all[rows, :] = z_sum(gram, gram_z, gram_copies)
    gram_copies = gather_z(gram_all)
    q2_y[y % 2] = z_sum(q2, q2_z, q2_copies)
    q2_copies = [send(q2_y.at[y % 2], q2_y.at[y % 2], along_y[0])]
    x_sum(q10, q10_x, q10_copies)
    q10_copies = z_step(q10, q10_z)
    cap_copies = gather_core(cap_all, cap_copies)
    gram_copies = gather_x(gram_all, gram_copies)

    q10_own = z_sum(q10, q10_z, q10_copies)
    q1_own, q0_own = q10_own[:, 0:256], q10_own[:, 256:512]

    arrived(cap_copies)
    caps = cap_all[:, 0:512]
    cap2 = dot(pick(lambda i: slot_row(i // 4) + i % 4, N), caps)
    arrived(q2_copies)
    c2 = dot(jnp.concatenate([q2_y[1], q2_y[0]], axis=1), cap2, ((1,), (1,)))
    c2_all[rows, :] = c2
    c2_copies = gather_z(c2_all)
    gram_copies = gather_core(gram_all, gram_copies)
    cap1 = dot(pick(lambda i: slot_row((i % 128) // 2) + 4 + 2 * (i // 128) + i % 2, N), caps)

    arrived(gram_copies)
    q1_y[y % 4] = q1_own - dot(c2, gram_all[0:256, 0:256])
    q1_copies = [send(q1_y.at[y % 4], q1_y.at[y % 4], along_y[k]) for k in range(3)]
    q0_own = q0_own - dot(c2, gram_all[256:512, 0:256])
    caps = cap_all[:, 512:768]
    cap0 = jnp.concatenate(
        [dot(pick(lambda i: slot_row(i % 64) + 4 * s + i // 64, N), caps) for s in range(2)], axis=1
    )
    c2_copies = gather_x(c2_all, c2_copies)
    cross = jnp.concatenate([gram_all[0:256, 256:384], gram_all[256:512, 256:384]], axis=1)

    arrived(q1_copies)
    c1 = dot(
        jnp.concatenate([q1_y[2] + q1_y[3], q1_y[0] + q1_y[1]], axis=1), cap1, ((1,), (1,))
    )
    c1_all[rows, :] = c1
    q0_y[y] = q0_own - dot(c1, cross)
    q0_copies = [send(q0_y.at[y], q0_y.at[y], along_y[k]) for k in range(7)]
    c1_copies = gather_z(c1_all)
    c2_copies = gather_core(c2_all, c2_copies)
    c1_copies = gather_x(c1_all, c1_copies)

    arrived(q0_copies)
    c0 = dot(
        jnp.concatenate(
            [(q0_y[4] + q0_y[5]) + (q0_y[6] + q0_y[7]), (q0_y[0] + q0_y[1]) + (q0_y[2] + q0_y[3])],
            axis=1,
        ),
        cap0,
        ((1,), (1,)),
    )
    c0_all[rows, :] = c0
    c0_copies = gather_z(c0_all)
    arrived(c2_copies)
    state = x_ref[...] - dot(w2_ref[...], c2_all[...], ((1,), (1,)))
    c1_copies = gather_core(c1_all, c1_copies)
    c0_copies = gather_x(c0_all, c0_copies)
    arrived(c1_copies)
    state = state - dot(w1_ref[...], c1_all[...], ((1,), (1,)))
    c0_copies = gather_core(c0_all, c0_copies)
    arrived(c0_copies)
    out_ref[...] = state - dot(w0_ref[...], c0_all[...], ((1,), (1,)))
    for copy in started:
        copy.wait_send()


def shards(
    rhs, v_basis0, w_basis0, cap_inv0, v_basis1, w_basis1, cap_inv1, v_basis2, w_basis2, cap_inv2
):
    vmem = pl.BlockSpec(memory_space=pltpu.VMEM)
    copies = 180

    def f32(*shape):
        return pltpu.VMEM(shape, F32)

    return pl.pallas_call(
        kernel,
        out_shape=jax.ShapeDtypeStruct(rhs.shape, F32),
        in_specs=[vmem] * 10,
        out_specs=vmem,
        scratch_shapes=[
            f32(512, 384), f32(512, 256), f32(512, 512),
            f32(256, 384), f32(256, 256), f32(256, 512),
            f32(3, 64, 384), f32(3, 64, 256), f32(3, 64, 512),
            f32(7, 8, 384), f32(7, 8, 256), f32(7, 8, 512),
            f32(512, 384), f32(512, 768), f32(512, 256), f32(512, 256), f32(512, 256),
            f32(2, 2, 512), f32(4, 1, 512), f32(2, 8, 256), f32(4, 8, 256), f32(8, 8, 256),
            pltpu.SemaphoreType.DMA((copies,)),
            pltpu.SemaphoreType.DMA((copies,)),
        ],
        compiler_params=pltpu.CompilerParams(
            collective_id=0, has_side_effects=True, vmem_limit_bytes=48 << 20
        ),
    )(rhs, v_basis0, w_basis0, cap_inv0, v_basis1, w_basis1, cap_inv1, v_basis2, w_basis2, cap_inv2)


def solution(mesh):
    rows = P("rows", None)
    return jax.shard_map(
        shards, mesh=mesh, in_specs=(rows,) * 10, out_specs=rows, check_vma=False
    )
```

```python
import jax
import jax.numpy as jnp
from jax import lax
from jax.experimental import pallas as pl
from jax.experimental.pallas import tpu as pltpu
from jax.sharding import PartitionSpec as P

MESH = pl.DeviceIdType.MESH
F32, BF16 = jnp.float32, jnp.bfloat16
NX, NZ, NC, NY = 4, 8, 2, 8
K, N, R = 256, 512, 8


def split(a):
    high = a.astype(BF16)
    return high, (a - high.astype(F32)).astype(BF16)


def part(a, b, dims):
    return lax.dot_general(a, b, (dims, ((), ())), preferred_element_type=F32)


def dot(a, b, dims=((1,), (0,))):
    (a_high, a_low), (b_high, b_low) = a, b
    return part(a_high, b_high, dims) + (part(a_high, b_low, dims) + part(a_low, b_high, dims))


def few_rows_dot(a, b, dims=((1,), (0,))):
    (a_high, a_low), (b_high, b_low) = split(a), b
    both = part(jnp.concatenate([a_high, a_low], axis=0), b_high, dims)
    return both[0:R] + (both[R:] + part(a_high, b_low, dims))


def pick(count, rows_of, pieces):
    row = lax.broadcasted_iota(jnp.int32, (count, N), 0)
    column = lax.broadcasted_iota(jnp.int32, (count, N), 1)
    chosen = (column == rows_of(row)).astype(F32).astype(BF16)
    return part(chosen, pieces, ((1,), (0,))).astype(BF16)


def paired_rows(rows_of, first, second):
    pieces = jnp.concatenate(split(jnp.concatenate([first, second], axis=1)), axis=1)
    quarters = [pick(128, lambda i: rows_of(i) + q, pieces) for q in range(4)]

    def matrix(start):
        upper = jnp.concatenate([q[:, start : start + 128] for q in quarters], axis=1)
        lower = jnp.concatenate([q[:, start + 128 : start + 256] for q in quarters], axis=1)
        return jnp.concatenate([upper, lower], axis=0)

    return matrix(0), matrix(256)


def slot_row(member):
    return 8 * ((member % 2) * 32 + member // 2)


def kernel(
    x_hbm, v0_hbm, w0_hbm, cap0_hbm, v1_hbm, w1_hbm, cap1_hbm, v2_hbm, w2_hbm, cap2_hbm,
    out_ref,
    x_ref, v0_ref, w0_ref, cap0_ref, v1_ref, w1_ref, cap1_ref, v2_ref, w2_ref, cap2_ref, load_sem,
    gram, gram_c, gram_z, gram_x, gram_all,
    q2, cross, q10, q2_c, cross_c, q10_c, q2_x, cross_x, q10_x, q2_z, cross_z, q10_z,
    cross_all, cap2_all, cap10_all, cap10_y, c2_all, c1_all, c0_all,
    cap0_y, q2_y, q1_y, q0_y,
    send_sem, recv_sem,
):
    me = lax.axis_index("rows")
    y, x, z, c = me // 64, (me // 16) % 4, (me // 2) % 8, me % 2
    other = 1 - c
    half = pl.multiple_of(c * 256, 256)
    other_half = pl.multiple_of(other * 256, 256)
    block = pl.multiple_of(c * 256 + x * 64, 64)
    own = pl.multiple_of(c * 256 + x * 64 + z * 8, 8)

    def at(yy, xx, zz, cc):
        return ((yy * 4 + xx) * 8 + zz) * 2 + cc

    def flip(k):
        b0, b1, b2 = y % 2, (y // 2) % 2, y // 4
        b0 = 1 - b0 if k & 1 else b0
        b1 = 1 - b1 if k & 2 else b1
        b2 = 1 - b2 if k & 4 else b2
        return b2 * 4 + b1 * 2 + b0

    core = at(y, x, z, other)
    along_x = [((x + k) % 4, at(y, (x + k) % 4, z, c)) for k in range(1, 4)]
    along_z = [((z + k) % 8, at(y, x, (z + k) % 8, c)) for k in range(1, 8)]
    along_y = [at(flip(k), x, z, c) for k in range(1, 8)]

    barrier = pltpu.get_barrier_semaphore()
    everyone = [core] + [d for _, d in along_x] + [d for _, d in along_z] + along_y
    for device in everyone:
        pl.semaphore_signal(barrier, inc=1, device_id=(device,), device_id_type=MESH)

    loads = {}
    for index, (name, source, target) in enumerate(
        [
            ("w2", w2_hbm, w2_ref), ("v1", v1_hbm, v1_ref), ("cap2", cap2_hbm, cap2_ref),
            ("cap0", cap0_hbm, cap0_ref), ("cap1", cap1_hbm, cap1_ref), ("x", x_hbm, x_ref),
            ("v2", v2_hbm, v2_ref), ("v0", v0_hbm, v0_ref), ("w1", w1_hbm, w1_ref),
            ("w0", w0_hbm, w0_ref),
        ]
    ):
        loads[name] = pltpu.make_async_copy(source, target, load_sem.at[index])
        loads[name].start()

    used = [0]
    sent = []

    def group(moves, size_like):
        index = used[0]
        used[0] += 1
        for source, target, device in moves:
            pltpu.make_async_remote_copy(
                src_ref=source,
                dst_ref=target,
                send_sem=send_sem.at[index],
                recv_sem=recv_sem.at[index],
                device_id=(device,),
                device_id_type=MESH,
            ).start()
        sent.append((index, size_like))
        return index, size_like

    def arrived(one_group):
        index, size_like = one_group
        pltpu.make_async_copy(size_like, size_like, recv_sem.at[index]).wait()

    def left():
        for index, size_like in sent:
            pltpu.make_async_copy(size_like, size_like, send_sem.at[index]).wait()
        sent.clear()

    def core_step(buffer, landing):
        return group([(buffer.at[pl.ds(other_half, 256)], landing, core)], landing)

    def core_sum(buffer, landing, copies):
        arrived(copies)
        buffer[pl.ds(half, 256), :] += landing[...]

    def x_step(buffer, landing):
        return group(
            [
                (
                    buffer.at[pl.ds(pl.multiple_of(c * 256 + xx * 64, 64), 64)],
                    landing.at[k],
                    device,
                )
                for k, (xx, device) in enumerate(along_x)
            ],
            landing,
        )

    def x_sum(buffer, landing, copies):
        arrived(copies)
        buffer[pl.ds(block, 64), :] += landing[0] + landing[1] + landing[2]

    def z_step(buffer, landing):
        return group(
            [
                (
                    buffer.at[pl.ds(pl.multiple_of(c * 256 + x * 64 + zz * 8, 8), 8)],
                    landing.at[k],
                    device,
                )
                for k, (zz, device) in enumerate(along_z)
            ],
            landing,
        )

    def z_sum(buffer, landing, copies):
        arrived(copies)
        total = buffer[pl.ds(own, 8), :]
        for k in range(7):
            total = total + landing[k]
        return total

    def gather_z(full):
        piece = full.at[pl.ds(own, 8)]
        return group([(piece, piece, device) for _, device in along_z], full.at[pl.ds(0, 56)])

    def gather_x(full, copies):
        arrived(copies)
        piece = full.at[pl.ds(block, 64)]
        return group([(piece, piece, device) for _, device in along_x], full.at[pl.ds(0, 192)])

    def gather_core(full, copies):
        arrived(copies)
        piece = full.at[pl.ds(half, 256)]
        return group([(piece, piece, core)], piece)

    def exchange_y(slots, mine, count):
        piece = slots.at[mine]
        return group([(piece, piece, along_y[k]) for k in range(count)], slots.at[pl.ds(0, count)])

    rows = pl.ds(own, 8)
    half_rows = pl.ds(half, 256)
    gram_half = pl.ds(pl.multiple_of(c * 128, 128), 128)
    gram_rows = pl.ds(pl.multiple_of(c * 128 + z * 16, 16), 16)

    loads["w2"].wait()
    loads["v1"].wait()
    w2_t, v1 = split(w2_ref[...].T), split(v1_ref[...])
    gram[...] = dot(w2_t, v1)
    loads["cap2"].wait()
    cap2_all[rows, :] = jnp.concatenate([cap2_ref[:, 0:256], cap2_ref[:, 256:512]], axis=0)
    loads["cap0"].wait()
    cap0_y[y % 2] = cap0_ref[...]

    pl.semaphore_wait(barrier, len(everyone))
    gram_copies = group(
        [(gram.at[pl.ds(pl.multiple_of(other * 128, 128), 128)], gram_c, core)], gram_c
    )
    cap2_copies = gather_z(cap2_all)
    cap0_copies = group([(cap0_ref, cap0_y.at[y % 2], along_y[0])], cap0_ref)

    loads["v0"].wait()
    loads["w1"].wait()
    v0 = split(v0_ref[...])
    cross[0:256, :] = dot(w2_t, v0)
    cross[256:512, :] = dot(split(w1_ref[...].T), v0)
    cross_copies = core_step(cross, cross_c)

    arrived(gram_copies)
    gram[gram_half, :] += gram_c[...]
    gram_copies = group(
        [
            (gram.at[pl.ds(pl.multiple_of(c * 128 + zz * 16, 16), 16)], gram_z.at[k], device)
            for k, (zz, device) in enumerate(along_z)
        ],
        gram_z,
    )

    loads["x"].wait()
    loads["v2"].wait()
    x_t = split(x_ref[...].T)
    q2[...] = dot(x_t, split(v2_ref[...]))
    q2_copies = core_step(q2, q2_c)

    core_sum(cross, cross_c, cross_copies)
    cross_copies = x_step(cross, cross_x)

    q10[:, 0:256] = dot(x_t, v1)
    core_sum(q2, q2_c, q2_copies)
    q2_copies = x_step(q2, q2_x)
    q10[:, 256:512] = dot(x_t, v0)
    q10_copies = core_step(q10, q10_c)

    arrived(cap0_copies)
    loads["cap1"].wait()
    cap10_all[rows, 0:128] = jnp.concatenate(
        [cap1_ref[r : r + 1, 128 * q : 128 * q + 128] for r in range(2) for q in range(4)], axis=0
    )
    cap10_all[rows, 128:256] = jnp.concatenate(
        [cap0_y[r][:, 128 * q : 128 * q + 128] for r in range(2) for q in range(4)], axis=0
    )
    cap10_copies = gather_z(cap10_all)
    cap2_copies = gather_x(cap2_all, cap2_copies)

    arrived(gram_copies)
    total = gram[gram_rows, :]
    for k in range(7):
        total = total + gram_z[k]
    gram[gram_rows, :] = total
    gram_copies = group(
        [(gram.at[gram_rows], gram_x.at[k], device) for k, (_, device) in enumerate(along_x)],
        gram_x,
    )
    core_sum(q10, q10_c, q10_copies)
    x_sum(cross, cross_x, cross_copies)
    cross_copies = z_step(cross, cross_z)
    x_sum(q2, q2_x, q2_copies)
    q2_copies = z_step(q2, q2_z)
    q10_copies = x_step(q10, q10_x)

    arrived(gram_copies)
    gram_all[gram_rows, :] = total + (gram_x[0] + gram_x[1] + gram_x[2])
    piece = gram_all.at[gram_rows]
    gram_copies = group(
        [(piece, piece, device) for _, device in along_z], gram_all.at[pl.ds(0, 112)]
    )
    cap2_copies = gather_core(cap2_all, cap2_copies)
    cross_all[rows, :] = z_sum(cross, cross_z, cross_copies)
    cross_copies = gather_z(cross_all)
    q2_y[y % 2] = z_sum(q2, q2_z, q2_copies)
    q2_copies = exchange_y(q2_y, y % 2, 1)
    cap10_copies = gather_x(cap10_all, cap10_copies)

    arrived(cap2_copies)
    pieces = jnp.concatenate(split(cap2_all[...]), axis=1)
    halves = [
        pick(256, lambda i: slot_row(i // 4) + i % 4 + 4 * h, pieces) for h in range(2)
    ]
    cap2 = tuple(
        jnp.concatenate([h[:, k : k + 256] for h in halves], axis=1) for k in (0, 256)
    )
    x_sum(q10, q10_x, q10_copies)
    q10_copies = z_step(q10, q10_z)

    arrived(q2_copies)
    c2 = few_rows_dot(jnp.concatenate([q2_y[1], q2_y[0]], axis=1), cap2, ((1,), (1,)))
    c2_all[rows, :] = c2
    c2_copies = gather_z(c2_all)
    arrived(gram_copies)
    piece = gram_all.at[gram_half]
    gram_copies = group([(piece, piece, core)], piece)
    cross_copies = gather_x(cross_all, cross_copies)
    arrived(cap10_copies)
    cap10_copies = group(
        [
            (cap10_all.at[half_rows, 0:128], cap10_y.at[half_rows, 0:128], along_y[0]),
            (cap10_all.at[half_rows, 128:256], cap10_y.at[half_rows, 128:256], along_y[1]),
        ],
        cap10_y.at[half_rows],
    )
    arrived(gram_copies)
    step = few_rows_dot(c2, split(gram_all[...]))
    q10_own = z_sum(q10, q10_z, q10_copies)
    q1_y[y % 4] = q10_own[:, 0:256] - step
    q1_copies = exchange_y(q1_y, y % 4, 3)

    c2_copies = gather_x(c2_all, c2_copies)
    arrived(cap10_copies)
    cap10_copies = group(
        [(b.at[half_rows], b.at[half_rows], core) for b in (cap10_all, cap10_y)], cap10_all
    )
    cross_copies = gather_core(cross_all, cross_copies)
    arrived(cap10_copies)
    even, even_pair = y % 2 == 0, (y // 2) % 2 == 0
    mine, theirs = cap10_all[:, 0:128], cap10_y[:, 0:128]
    cap1 = paired_rows(
        lambda i: slot_row(i // 2) + 4 * (i % 2),
        jnp.where(even, mine, theirs),
        jnp.where(even, theirs, mine),
    )

    arrived(q1_copies)
    c1 = few_rows_dot(
        jnp.concatenate([q1_y[2] + q1_y[3], q1_y[0] + q1_y[1]], axis=1), cap1, ((1,), (1,))
    )
    c1_all[rows, :] = c1
    arrived(cross_copies)
    q0_y[y] = q10_own[:, 256:512] - few_rows_dot(
        jnp.concatenate([c2, c1], axis=1), split(cross_all[...])
    )
    q0_copies = exchange_y(q0_y, y, 7)
    c1_copies = gather_z(c1_all)
    mine, theirs = cap10_all[:, 128:256], cap10_y[:, 128:256]
    cap0 = paired_rows(
        lambda i: slot_row(i % 64) + 4 * (i // 64),
        jnp.where(even_pair, mine, theirs),
        jnp.where(even_pair, theirs, mine),
    )
    c2_copies = gather_core(c2_all, c2_copies)

    arrived(q0_copies)
    c0 = few_rows_dot(
        jnp.concatenate(
            [(q0_y[4] + q0_y[5]) + (q0_y[6] + q0_y[7]), (q0_y[0] + q0_y[1]) + (q0_y[2] + q0_y[3])],
            axis=1,
        ),
        cap0,
        ((1,), (1,)),
    )
    c0_all[rows, :] = c0
    c0_copies = gather_z(c0_all)
    c1_copies = gather_x(c1_all, c1_copies)
    arrived(c2_copies)
    out_ref[...] = x_ref[...] - dot(split(w2_ref[...]), split(c2_all[...]), ((1,), (1,)))
    c0_copies = gather_x(c0_all, c0_copies)
    c1_copies = gather_core(c1_all, c1_copies)
    arrived(c1_copies)
    out_ref[...] -= dot(split(w1_ref[...]), split(c1_all[...]), ((1,), (1,)))
    loads["w0"].wait()
    w0 = split(w0_ref[...])
    left()
    c0_copies = gather_core(c0_all, c0_copies)
    out_ref[:, half_rows] -= dot(w0, split(c0_all[half_rows, :]), ((1,), (1,)))
    arrived(c0_copies)
    half_rows = pl.ds(other_half, 256)
    out_ref[:, half_rows] -= dot(w0, split(c0_all[half_rows, :]), ((1,), (1,)))
    left()


def shards(
    rhs, v_basis0, w_basis0, cap_inv0, v_basis1, w_basis1, cap_inv1, v_basis2, w_basis2, cap_inv2
):
    groups = 37

    def f32(*shape):
        return pltpu.VMEM(shape, F32)

    return pl.pallas_call(
        kernel,
        out_shape=jax.ShapeDtypeStruct(rhs.shape, F32),
        in_specs=[pl.BlockSpec(memory_space=pltpu.HBM)] * 10,
        out_specs=pl.BlockSpec(memory_space=pltpu.VMEM),
        scratch_shapes=[
            f32(256, 512), f32(256, 256), f32(256, 256), f32(1, 512), f32(256, 256),
            f32(256, 256), f32(2, 512), f32(256, 256), f32(256, 256), f32(4, 512),
            pltpu.SemaphoreType.DMA((10,)),
            f32(256, 256), f32(128, 256), f32(7, 16, 256), f32(3, 16, 256), f32(256, 256),
            f32(512, 256), f32(512, 256), f32(512, 512),
            f32(256, 256), f32(256, 256), f32(256, 512),
            f32(3, 64, 256), f32(3, 64, 256), f32(3, 64, 512),
            f32(7, 8, 256), f32(7, 8, 256), f32(7, 8, 512),
            f32(512, 256), f32(512, 256), f32(512, 256), f32(512, 256),
            f32(512, 256), f32(512, 256), f32(512, 256),
            f32(2, 1, 512), f32(2, 8, 256), f32(4, 8, 256), f32(8, 8, 256),
            pltpu.SemaphoreType.DMA((groups,)),
            pltpu.SemaphoreType.DMA((groups,)),
        ],
        compiler_params=pltpu.CompilerParams(
            collective_id=0, has_side_effects=True, vmem_limit_bytes=52000 * 1024
        ),
    )(
        *(
            pltpu.with_memory_space_constraint(argument, pltpu.HBM)
            for argument in (
                rhs, v_basis0, w_basis0, cap_inv0, v_basis1, w_basis1, cap_inv1,
                v_basis2, w_basis2, cap_inv2,
            )
        )
    )


def solution(mesh):
    rows = P("rows", None)
    return jax.shard_map(
        shards, mesh=mesh, in_specs=(rows,) * 10, out_specs=rows, check_vma=False
    )
```

```python
import math

import jax
import jax.numpy as jnp
from jax import lax
from jax.experimental import pallas as pl
from jax.experimental.pallas import tpu as pltpu
from jax.sharding import PartitionSpec as P

MESH = pl.DeviceIdType.MESH
F32, BF16 = jnp.float32, jnp.bfloat16
NX, NZ, NC, NY = 4, 8, 2, 8
K, N, R = 256, 512, 8


def split(a):
    high = a.astype(BF16)
    return high, (a - high.astype(F32)).astype(BF16)


def part(a, b, dims):
    return lax.dot_general(a, b, (dims, ((), ())), preferred_element_type=F32)


def dot(a, b, dims=((1,), (0,))):
    (a_high, a_low), (b_high, b_low) = a, b
    return part(a_high, b_high, dims) + (part(a_high, b_low, dims) + part(a_low, b_high, dims))


def few_rows_dot(a, b, dims=((1,), (0,))):
    (a_high, a_low), (b_high, b_low) = split(a), b
    both = part(jnp.concatenate([a_high, a_low], axis=0), b_high, dims)
    return both[0:R] + (both[R:] + part(a_high, b_low, dims))


def pick(count, rows_of, pieces):
    row = lax.broadcasted_iota(jnp.int32, (count, N), 0)
    column = lax.broadcasted_iota(jnp.int32, (count, N), 1)
    chosen = (column == rows_of(row)).astype(F32).astype(BF16)
    return part(chosen, pieces, ((1,), (0,))).astype(BF16)


def paired_rows(rows_of, first, second):
    pieces = jnp.concatenate(split(jnp.concatenate([first, second], axis=1)), axis=1)
    quarters = [pick(128, lambda i: rows_of(i) + q, pieces) for q in range(4)]

    def matrix(start):
        upper = jnp.concatenate([q[:, start : start + 128] for q in quarters], axis=1)
        lower = jnp.concatenate([q[:, start + 128 : start + 256] for q in quarters], axis=1)
        return jnp.concatenate([upper, lower], axis=0)

    return matrix(0), matrix(256)


def slot_row(member):
    return 8 * ((member % 2) * 32 + member // 2)


def kernel(
    x_hbm, v0_hbm, w0_hbm, cap0_hbm, v1_hbm, w1_hbm, cap1_hbm, v2_hbm, w2_hbm, cap2_hbm,
    out_ref,
    x_ref, v0_ref, w0_ref, cap0_ref, v1_ref, w1_ref, cap1_ref, v2_ref, w2_ref, cap2_ref, load_sem,
    gram, gram_c, gram_z, gram_x, gram_all,
    q2, cross, q1, q0, q2_c, cross_c, q1_c, q0_c, q2_x, cross_x, q1_x, q0_x,
    q2_z, cross_z, q1_z, q0_z,
    cross_all, cap2_all, cap10_all, cap10_y, c2_all, c1_all, c0_all,
    cap0_y, q2_y, q1_y, q0_y,
    all_sent, send_sem, recv_sem,
):
    me = lax.axis_index("rows")
    y, x, z, c = me // 64, (me // 16) % 4, (me // 2) % 8, me % 2
    other = 1 - c
    half = pl.multiple_of(c * 256, 256)
    other_half = pl.multiple_of(other * 256, 256)
    block = pl.multiple_of(c * 256 + x * 64, 64)
    own = pl.multiple_of(c * 256 + x * 64 + z * 8, 8)

    def at(yy, xx, zz, cc):
        return ((yy * 4 + xx) * 8 + zz) * 2 + cc

    def flip(k):
        b0, b1, b2 = y % 2, (y // 2) % 2, y // 4
        b0 = 1 - b0 if k & 1 else b0
        b1 = 1 - b1 if k & 2 else b1
        b2 = 1 - b2 if k & 4 else b2
        return b2 * 4 + b1 * 2 + b0

    core = at(y, x, z, other)
    along_x = [((x + k) % 4, at(y, (x + k) % 4, z, c)) for k in (2, 1, 3)]
    along_z = [((z + k) % 8, at(y, x, (z + k) % 8, c)) for k in (4, 3, 5, 2, 6, 1, 7)]
    along_y = {k: at(flip(k), x, z, c) for k in (4, 5, 3, 6, 2, 7, 1)}

    barrier = pltpu.get_barrier_semaphore()
    everyone = [core] + [d for _, d in along_x] + [d for _, d in along_z] + list(along_y.values())
    for device in everyone:
        pl.semaphore_signal(barrier, inc=1, device_id=(device,), device_id_type=MESH)

    loads = {}
    for index, (name, source, target) in enumerate(
        [
            ("w2", w2_hbm, w2_ref), ("v0", v0_hbm, v0_ref), ("w1", w1_hbm, w1_ref),
            ("cap0", cap0_hbm, cap0_ref), ("cap2", cap2_hbm, cap2_ref), ("v1", v1_hbm, v1_ref),
            ("x", x_hbm, x_ref), ("v2", v2_hbm, v2_ref), ("cap1", cap1_hbm, cap1_ref),
            ("w0", w0_hbm, w0_ref),
        ]
    ):
        loads[name] = pltpu.make_async_copy(source, target, load_sem.at[index])
        loads[name].start()

    used = [0]
    sent = [0]

    def group(moves, size_like):
        index = used[0]
        used[0] += 1
        size = math.prod(size_like.shape) // K
        bucket = len(sent) - 1 if size >= 8 else send_sem.shape[0] - 1
        if size >= 8 and sent[-1] + size > all_sent.shape[0]:
            bucket = len(sent)
            sent.append(0)
        if size >= 8:
            sent[bucket] += size
        for source, target, device in moves:
            pltpu.make_async_remote_copy(
                src_ref=source,
                dst_ref=target,
                send_sem=send_sem.at[bucket],
                recv_sem=recv_sem.at[index],
                device_id=(device,),
                device_id_type=MESH,
            ).start()
        return index, size_like

    def arrived(one_group):
        index, size_like = one_group
        pltpu.make_async_copy(size_like, size_like, recv_sem.at[index]).wait()

    def left():
        for index, size in enumerate(sent):
            amount = all_sent.at[pl.ds(0, size)]
            pltpu.make_async_copy(amount, amount, send_sem.at[index]).wait()
        pltpu.make_async_copy(cap0_ref, cap0_ref, send_sem.at[send_sem.shape[0] - 1]).wait()

    def core_step(buffer, landing):
        return group([(buffer.at[pl.ds(other_half, 256)], landing, core)], landing)

    def core_sum(buffer, landing, copies):
        arrived(copies)
        buffer[pl.ds(half, 256), :] += landing[...]

    def x_step(buffer, landing):
        return group(
            [
                (
                    buffer.at[pl.ds(pl.multiple_of(c * 256 + xx * 64, 64), 64)],
                    landing.at[k],
                    device,
                )
                for k, (xx, device) in enumerate(along_x)
            ],
            landing,
        )

    def x_sum(buffer, landing, copies):
        arrived(copies)
        buffer[pl.ds(block, 64), :] += landing[0] + landing[1] + landing[2]

    def z_step(buffer, landing):
        return group(
            [
                (
                    buffer.at[pl.ds(pl.multiple_of(c * 256 + x * 64 + zz * 8, 8), 8)],
                    landing.at[k],
                    device,
                )
                for k, (zz, device) in enumerate(along_z)
            ],
            landing,
        )

    def z_sum(buffer, landing, copies):
        arrived(copies)
        total = buffer[pl.ds(own, 8), :]
        for k in range(7):
            total = total + landing[k]
        return total

    def gather_z(full):
        piece = full.at[pl.ds(own, 8)]
        return group([(piece, piece, device) for _, device in along_z], full.at[pl.ds(0, 56)])

    def gather_x(full, copies):
        arrived(copies)
        piece = full.at[pl.ds(block, 64)]
        return group([(piece, piece, device) for _, device in along_x], full.at[pl.ds(0, 192)])

    def gather_core(full, copies):
        arrived(copies)
        piece = full.at[pl.ds(half, 256)]
        return group([(piece, piece, core)], piece)

    def exchange_y(slots, mine, count):
        piece = slots.at[mine]
        devices = [device for k, device in along_y.items() if k <= count]
        return group([(piece, piece, device) for device in devices], slots.at[pl.ds(0, count)])

    rows = pl.ds(own, 8)
    half_rows = pl.ds(half, 256)
    gram_half = pl.ds(pl.multiple_of(c * 128, 128), 128)
    gram_rows = pl.ds(pl.multiple_of(c * 128 + z * 16, 16), 16)

    loads["w2"].wait()
    loads["v0"].wait()
    w2_t, v0 = split(w2_ref[...].T), split(v0_ref[...])
    cross[0:256, :] = dot(w2_t, v0)
    loads["w1"].wait()
    cross[256:512, :] = dot(split(w1_ref[...].T), v0)
    loads["cap0"].wait()
    cap0_y[y % 2] = cap0_ref[...]
    loads["cap2"].wait()
    cap2_all[rows, :] = jnp.concatenate([cap2_ref[:, 0:256], cap2_ref[:, 256:512]], axis=0)

    pl.semaphore_wait(barrier, len(everyone))
    cross_copies = core_step(cross, cross_c)
    cap0_copies = group([(cap0_ref, cap0_y.at[y % 2], along_y[1])], cap0_ref)
    cap2_copies = gather_z(cap2_all)

    loads["v1"].wait()
    v1 = split(v1_ref[...])
    gram[...] = dot(w2_t, v1)
    gram_copies = group(
        [(gram.at[pl.ds(pl.multiple_of(other * 128, 128), 128)], gram_c, core)], gram_c
    )
    core_sum(cross, cross_c, cross_copies)
    cross_copies = x_step(cross, cross_x)

    loads["x"].wait()
    loads["v2"].wait()
    x_t = split(x_ref[...].T)
    q2[...] = dot(x_t, split(v2_ref[...]))
    q2_copies = core_step(q2, q2_c)

    arrived(gram_copies)
    gram[gram_half, :] += gram_c[...]
    gram_copies = group(
        [
            (gram.at[pl.ds(pl.multiple_of(c * 128 + zz * 16, 16), 16)], gram_z.at[k], device)
            for k, (zz, device) in enumerate(along_z)
        ],
        gram_z,
    )

    arrived(cap0_copies)
    loads["cap1"].wait()
    cap10_all[rows, 0:128] = jnp.concatenate(
        [cap1_ref[r : r + 1, 128 * q : 128 * q + 128] for r in range(2) for q in range(4)], axis=0
    )
    cap10_all[rows, 128:256] = jnp.concatenate(
        [cap0_y[r][:, 128 * q : 128 * q + 128] for r in range(2) for q in range(4)], axis=0
    )
    cap10_copies = gather_z(cap10_all)

    core_sum(q2, q2_c, q2_copies)
    q2_copies = x_step(q2, q2_x)
    q1[...] = dot(x_t, v1)
    q1_copies = core_step(q1, q1_c)
    cap2_copies = gather_x(cap2_all, cap2_copies)
    x_sum(cross, cross_x, cross_copies)
    cross_copies = z_step(cross, cross_z)
    q0[...] = dot(x_t, v0)
    q0_copies = core_step(q0, q0_c)

    arrived(gram_copies)
    total = gram[gram_rows, :]
    for k in range(7):
        total = total + gram_z[k]
    gram[gram_rows, :] = total
    gram_copies = group(
        [(gram.at[gram_rows], gram_x.at[k], device) for k, (_, device) in enumerate(along_x)],
        gram_x,
    )
    cap10_copies = gather_x(cap10_all, cap10_copies)
    x_sum(q2, q2_x, q2_copies)
    q2_copies = z_step(q2, q2_z)
    core_sum(q1, q1_c, q1_copies)
    q1_copies = x_step(q1, q1_x)
    core_sum(q0, q0_c, q0_copies)

    cross_all[rows, :] = z_sum(cross, cross_z, cross_copies)
    cross_copies = gather_z(cross_all)
    arrived(gram_copies)
    gram_all[gram_rows, :] = total + (gram_x[0] + gram_x[1] + gram_x[2])
    piece = gram_all.at[gram_rows]
    gram_copies = group(
        [(piece, piece, device) for _, device in along_z], gram_all.at[pl.ds(0, 112)]
    )
    q0_copies = x_step(q0, q0_x)
    cap2_copies = gather_core(cap2_all, cap2_copies)
    q2_y[y % 2] = z_sum(q2, q2_z, q2_copies)
    q2_copies = exchange_y(q2_y, y % 2, 1)
    arrived(cap10_copies)
    cap10_copies = group(
        [
            (cap10_all.at[half_rows, 0:128], cap10_y.at[half_rows, 0:128], along_y[1]),
            (cap10_all.at[half_rows, 128:256], cap10_y.at[half_rows, 128:256], along_y[2]),
        ],
        cap10_y.at[half_rows],
    )
    x_sum(q1, q1_x, q1_copies)
    q1_copies = z_step(q1, q1_z)

    arrived(cap2_copies)
    pieces = jnp.concatenate(split(cap2_all[...]), axis=1)
    halves = [
        pick(256, lambda i: slot_row(i // 4) + i % 4 + 4 * h, pieces) for h in range(2)
    ]
    cap2 = tuple(
        jnp.concatenate([h[:, k : k + 256] for h in halves], axis=1) for k in (0, 256)
    )
    cross_copies = gather_x(cross_all, cross_copies)
    arrived(q2_copies)
    c2 = few_rows_dot(jnp.concatenate([q2_y[1], q2_y[0]], axis=1), cap2, ((1,), (1,)))
    c2_all[rows, :] = c2
    arrived(gram_copies)
    piece = gram_all.at[gram_half]
    gram_copies = group([(piece, piece, core)], piece)
    arrived(cap10_copies)
    cap10_copies = group(
        [(b.at[half_rows], b.at[half_rows], core) for b in (cap10_all, cap10_y)], cap10_all
    )
    x_sum(q0, q0_x, q0_copies)
    q0_copies = z_step(q0, q0_z)
    q1_own = z_sum(q1, q1_z, q1_copies)
    arrived(gram_copies)
    q1_y[y % 4] = q1_own - few_rows_dot(c2, split(gram_all[...]))
    q1_copies = exchange_y(q1_y, y % 4, 3)
    c2_copies = gather_z(c2_all)
    cross_copies = gather_core(cross_all, cross_copies)

    arrived(cap10_copies)
    even, even_pair = y % 2 == 0, (y // 2) % 2 == 0
    mine, theirs = cap10_all[:, 0:128], cap10_y[:, 0:128]
    cap1 = paired_rows(
        lambda i: slot_row(i // 2) + 4 * (i % 2),
        jnp.where(even, mine, theirs),
        jnp.where(even, theirs, mine),
    )
    arrived(cross_copies)
    cross_high, cross_low = split(cross_all[...])
    q0_own = z_sum(q0, q0_z, q0_copies)
    q0_own = q0_own - few_rows_dot(c2, (cross_high[0:256], cross_low[0:256]))

    arrived(q1_copies)
    c1 = few_rows_dot(
        jnp.concatenate([q1_y[2] + q1_y[3], q1_y[0] + q1_y[1]], axis=1), cap1, ((1,), (1,))
    )
    c1_all[rows, :] = c1
    q0_y[y] = q0_own - few_rows_dot(c1, (cross_high[256:512], cross_low[256:512]))
    q0_copies = exchange_y(q0_y, y, 7)
    c1_copies = gather_z(c1_all)
    c2_copies = gather_x(c2_all, c2_copies)
    mine, theirs = cap10_all[:, 128:256], cap10_y[:, 128:256]
    cap0 = paired_rows(
        lambda i: slot_row(i % 64) + 4 * (i // 64),
        jnp.where(even_pair, mine, theirs),
        jnp.where(even_pair, theirs, mine),
    )
    c2_copies = gather_core(c2_all, c2_copies)

    arrived(q0_copies)
    c0 = few_rows_dot(
        jnp.concatenate(
            [(q0_y[4] + q0_y[5]) + (q0_y[6] + q0_y[7]), (q0_y[0] + q0_y[1]) + (q0_y[2] + q0_y[3])],
            axis=1,
        ),
        cap0,
        ((1,), (1,)),
    )
    c0_all[rows, :] = c0
    c0_copies = gather_z(c0_all)
    c1_copies = gather_x(c1_all, c1_copies)
    arrived(c2_copies)
    out_ref[...] = x_ref[...] - dot(split(w2_ref[...]), split(c2_all[...]), ((1,), (1,)))
    c0_copies = gather_x(c0_all, c0_copies)
    c1_copies = gather_core(c1_all, c1_copies)
    arrived(c1_copies)
    out_ref[...] -= dot(split(w1_ref[...]), split(c1_all[...]), ((1,), (1,)))
    loads["w0"].wait()
    w0 = split(w0_ref[...])
    c0_copies = gather_core(c0_all, c0_copies)
    out_ref[:, half_rows] -= dot(w0, split(c0_all[half_rows, :]), ((1,), (1,)))
    arrived(c0_copies)
    half_rows = pl.ds(other_half, 256)
    out_ref[:, half_rows] -= dot(w0, split(c0_all[half_rows, :]), ((1,), (1,)))
    left()


def shards(
    rhs, v_basis0, w_basis0, cap_inv0, v_basis1, w_basis1, cap_inv1, v_basis2, w_basis2, cap_inv2
):
    groups = 40

    def f32(*shape):
        return pltpu.VMEM(shape, F32)

    return pl.pallas_call(
        kernel,
        out_shape=jax.ShapeDtypeStruct(rhs.shape, F32),
        in_specs=[pl.BlockSpec(memory_space=pltpu.HBM)] * 10,
        out_specs=pl.BlockSpec(memory_space=pltpu.VMEM),
        scratch_shapes=[
            f32(256, 512), f32(256, 256), f32(256, 256), f32(1, 512), f32(256, 256),
            f32(256, 256), f32(2, 512), f32(256, 256), f32(256, 256), f32(4, 512),
            pltpu.SemaphoreType.DMA((10,)),
            f32(256, 256), f32(128, 256), f32(7, 16, 256), f32(3, 16, 256), f32(256, 256),
            *[f32(512, 256)] * 4, *[f32(256, 256)] * 4, *[f32(3, 64, 256)] * 4, *[f32(7, 8, 256)] * 4,
            f32(512, 256), f32(512, 256), f32(512, 256), f32(512, 256),
            f32(512, 256), f32(512, 256), f32(512, 256),
            f32(2, 1, 512), f32(2, 8, 256), f32(4, 8, 256), f32(8, 8, 256),
            f32(1024, 256),
            pltpu.SemaphoreType.DMA((9,)),
            pltpu.SemaphoreType.DMA((groups,)),
        ],
        compiler_params=pltpu.CompilerParams(
            collective_id=0, has_side_effects=True, vmem_limit_bytes=52000 * 1024
        ),
    )(
        *(
            pltpu.with_memory_space_constraint(argument, pltpu.HBM)
            for argument in (
                rhs, v_basis0, w_basis0, cap_inv0, v_basis1, w_basis1, cap_inv1,
                v_basis2, w_basis2, cap_inv2,
            )
        )
    )


def solution(mesh):
    rows = P("rows", None)
    return jax.shard_map(
        shards, mesh=mesh, in_specs=(rows,) * 10, out_specs=rows, check_vma=False
    )
```

```python
import math

import jax
import jax.numpy as jnp
from jax import lax
from jax.experimental import pallas as pl
from jax.experimental.pallas import tpu as pltpu
from jax.sharding import PartitionSpec as P

MESH = pl.DeviceIdType.MESH
F32, BF16 = jnp.float32, jnp.bfloat16
NX, NZ, NC, NY = 4, 8, 2, 8
K, N, R = 256, 512, 8


def split(a):
    high = a.astype(BF16)
    return high, (a - high.astype(F32)).astype(BF16)


def part(a, b, dims):
    return lax.dot_general(a, b, (dims, ((), ())), preferred_element_type=F32)


def dot(a, b, dims=((1,), (0,))):
    (a_high, a_low), (b_high, b_low) = a, b
    return part(a_high, b_high, dims) + (part(a_high, b_low, dims) + part(a_low, b_high, dims))


def few_rows_dot(a, b, dims=((1,), (0,))):
    (a_high, a_low), (b_high, b_low) = split(a), b
    both = part(jnp.concatenate([a_high, a_low], axis=0), b_high, dims)
    return both[0:R] + (both[R:] + part(a_high, b_low, dims))


def pick(count, rows_of, pieces):
    row = lax.broadcasted_iota(jnp.int32, (count, N), 0)
    column = lax.broadcasted_iota(jnp.int32, (count, N), 1)
    chosen = (column == rows_of(row)).astype(F32).astype(BF16)
    return part(chosen, pieces, ((1,), (0,))).astype(BF16)


def paired_rows(rows_of, first, second):
    pieces = jnp.concatenate(split(jnp.concatenate([first, second], axis=1)), axis=1)
    quarters = [pick(128, lambda i: rows_of(i) + q, pieces) for q in range(4)]

    def matrix(start):
        upper = jnp.concatenate([q[:, start : start + 128] for q in quarters], axis=1)
        lower = jnp.concatenate([q[:, start + 128 : start + 256] for q in quarters], axis=1)
        return jnp.concatenate([upper, lower], axis=0)

    return matrix(0), matrix(256)


def slot_row(member):
    return 8 * ((member % 2) * 32 + member // 2)


def kernel(
    x_hbm, v0_hbm, w0_hbm, cap0_hbm, v1_hbm, w1_hbm, cap1_hbm, v2_hbm, w2_hbm, cap2_hbm,
    out_ref,
    x_ref, v0_ref, w0_ref, cap0_ref, v1_ref, w1_ref, cap1_ref, v2_ref, w2_ref, cap2_ref, load_sem,
    gram, gram_c, gram_z, gram_x, gram_all,
    q2, cross, q1, q0, q2_c, cross_c, q1_c, q0_c, q2_x, cross_x, q1_x, q0_x,
    q2_z, cross_z, q1_z, q0_z,
    cross_all, cap2_all, cap10_all, cap10_y, c2_all, c1_all, c0_all,
    cap0_y, q2_y, q1_y, q0_y,
    all_sent, send_sem, recv_sem,
):
    me = lax.axis_index("rows")
    y, x, z, c = me // 64, (me // 16) % 4, (me // 2) % 8, me % 2
    other = 1 - c
    half = pl.multiple_of(c * 256, 256)
    other_half = pl.multiple_of(other * 256, 256)
    block = pl.multiple_of(c * 256 + x * 64, 64)
    own = pl.multiple_of(c * 256 + x * 64 + z * 8, 8)

    def at(yy, xx, zz, cc):
        return ((yy * 4 + xx) * 8 + zz) * 2 + cc

    def flip(k):
        b0, b1, b2 = y % 2, (y // 2) % 2, y // 4
        b0 = 1 - b0 if k & 1 else b0
        b1 = 1 - b1 if k & 2 else b1
        b2 = 1 - b2 if k & 4 else b2
        return b2 * 4 + b1 * 2 + b0

    core = at(y, x, z, other)
    along_x = [((x + k) % 4, at(y, (x + k) % 4, z, c)) for k in (2, 1, 3)]
    along_z = [((z + k) % 8, at(y, x, (z + k) % 8, c)) for k in (4, 3, 5, 2, 6, 1, 7)]
    along_y = {k: at(flip(k), x, z, c) for k in (4, 5, 3, 6, 2, 7, 1)}

    barrier = pltpu.get_barrier_semaphore()
    everyone = [core] + [d for _, d in along_x] + [d for _, d in along_z] + list(along_y.values())
    for device in everyone:
        pl.semaphore_signal(barrier, inc=1, device_id=(device,), device_id_type=MESH)

    loads = {}
    for index, (name, source, target) in enumerate(
        [
            ("w2", w2_hbm, w2_ref), ("v0", v0_hbm, v0_ref), ("w1", w1_hbm, w1_ref),
            ("cap0", cap0_hbm, cap0_ref), ("cap2", cap2_hbm, cap2_ref), ("v1", v1_hbm, v1_ref),
            ("x", x_hbm, x_ref), ("v2", v2_hbm, v2_ref), ("cap1", cap1_hbm, cap1_ref),
            ("w0", w0_hbm, w0_ref),
        ]
    ):
        loads[name] = pltpu.make_async_copy(source, target, load_sem.at[index])
        loads[name].start()

    used = [0]
    sent = [0]

    def group(moves, size_like):
        index = used[0]
        used[0] += 1
        size = math.prod(size_like.shape) // K
        bucket = len(sent) - 1 if size >= 8 else send_sem.shape[0] - 1
        if size >= 8 and sent[-1] + size > all_sent.shape[0]:
            bucket = len(sent)
            sent.append(0)
        if size >= 8:
            sent[bucket] += size
        for source, target, device in moves:
            pltpu.make_async_remote_copy(
                src_ref=source,
                dst_ref=target,
                send_sem=send_sem.at[bucket],
                recv_sem=recv_sem.at[index],
                device_id=(device,),
                device_id_type=MESH,
            ).start()
        return index, size_like

    def arrived(one_group):
        index, size_like = one_group
        pltpu.make_async_copy(size_like, size_like, recv_sem.at[index]).wait()

    def left():
        for index, size in enumerate(sent):
            amount = all_sent.at[pl.ds(0, size)]
            pltpu.make_async_copy(amount, amount, send_sem.at[index]).wait()
        pltpu.make_async_copy(cap0_ref, cap0_ref, send_sem.at[send_sem.shape[0] - 1]).wait()

    def core_step(buffer, landing):
        return group([(buffer.at[pl.ds(other_half, 256)], landing, core)], landing)

    def core_sum(buffer, landing, copies):
        arrived(copies)
        buffer[pl.ds(half, 256), :] += landing[...]

    def x_step(buffer, landing):
        return group(
            [
                (
                    buffer.at[pl.ds(pl.multiple_of(c * 256 + xx * 64, 64), 64)],
                    landing.at[k],
                    device,
                )
                for k, (xx, device) in enumerate(along_x)
            ],
            landing,
        )

    def x_sum(buffer, landing, copies):
        arrived(copies)
        buffer[pl.ds(block, 64), :] += landing[0] + landing[1] + landing[2]

    def z_step(buffer, landing):
        return group(
            [
                (
                    buffer.at[pl.ds(pl.multiple_of(c * 256 + x * 64 + zz * 8, 8), 8)],
                    landing.at[k],
                    device,
                )
                for k, (zz, device) in enumerate(along_z)
            ],
            landing,
        )

    def z_sum(buffer, landing, copies):
        arrived(copies)
        total = buffer[pl.ds(own, 8), :]
        for k in range(7):
            total = total + landing[k]
        return total

    def gather_z(full):
        piece = full.at[pl.ds(own, 8)]
        return group([(piece, piece, device) for _, device in along_z], full.at[pl.ds(0, 56)])

    def gather_x(full, copies):
        arrived(copies)
        piece = full.at[pl.ds(block, 64)]
        return group([(piece, piece, device) for _, device in along_x], full.at[pl.ds(0, 192)])

    def gather_core(full, copies):
        arrived(copies)
        piece = full.at[pl.ds(half, 256)]
        return group([(piece, piece, core)], piece)

    def exchange_y(slots, mine, count):
        piece = slots.at[mine]
        devices = [device for k, device in along_y.items() if k <= count]
        return group([(piece, piece, device) for device in devices], slots.at[pl.ds(0, count)])

    rows = pl.ds(own, 8)
    half_rows = pl.ds(half, 256)
    gram_half = pl.ds(pl.multiple_of(c * 128, 128), 128)
    gram_rows = pl.ds(pl.multiple_of(c * 128 + z * 16, 16), 16)

    loads["w2"].wait()
    loads["v0"].wait()
    w2_t, v0 = split(w2_ref[...].T), split(v0_ref[...])
    cross[0:256, :] = dot(w2_t, v0)
    loads["w1"].wait()
    cross[256:512, :] = dot(split(w1_ref[...].T), v0)
    loads["cap0"].wait()
    cap0_y[y % 2] = cap0_ref[...]
    loads["cap2"].wait()
    cap2_all[rows, :] = jnp.concatenate([cap2_ref[:, 0:256], cap2_ref[:, 256:512]], axis=0)

    pl.semaphore_wait(barrier, len(everyone))
    cross_copies = core_step(cross, cross_c)
    cap0_copies = group([(cap0_ref, cap0_y.at[y % 2], along_y[1])], cap0_ref)
    cap2_copies = gather_z(cap2_all)

    loads["v1"].wait()
    v1 = split(v1_ref[...])
    gram[...] = dot(w2_t, v1)
    gram_copies = group(
        [(gram.at[pl.ds(pl.multiple_of(other * 128, 128), 128)], gram_c, core)], gram_c
    )
    core_sum(cross, cross_c, cross_copies)
    cross_copies = x_step(cross, cross_x)

    loads["x"].wait()
    loads["v2"].wait()
    x_t = split(x_ref[...].T)
    q2[...] = dot(x_t, split(v2_ref[...]))
    q2_copies = core_step(q2, q2_c)

    arrived(gram_copies)
    gram[gram_half, :] += gram_c[...]
    gram_copies = group(
        [
            (gram.at[pl.ds(pl.multiple_of(c * 128 + zz * 16, 16), 16)], gram_z.at[k], device)
            for k, (zz, device) in enumerate(along_z)
        ],
        gram_z,
    )

    arrived(cap0_copies)
    loads["cap1"].wait()
    cap10_all[rows, 0:128] = jnp.concatenate(
        [cap1_ref[r : r + 1, 128 * q : 128 * q + 128] for r in range(2) for q in range(4)], axis=0
    )
    cap10_all[rows, 128:256] = jnp.concatenate(
        [cap0_y[r][:, 128 * q : 128 * q + 128] for r in range(2) for q in range(4)], axis=0
    )
    cap10_copies = gather_z(cap10_all)

    core_sum(q2, q2_c, q2_copies)
    q2_copies = x_step(q2, q2_x)
    q1[...] = dot(x_t, v1)
    q1_copies = core_step(q1, q1_c)
    cap2_copies = gather_x(cap2_all, cap2_copies)
    x_sum(cross, cross_x, cross_copies)
    cross_copies = z_step(cross, cross_z)
    q0[...] = dot(x_t, v0)
    q0_copies = core_step(q0, q0_c)

    arrived(gram_copies)
    total = gram[gram_rows, :]
    for k in range(7):
        total = total + gram_z[k]
    gram[gram_rows, :] = total
    gram_copies = group(
        [(gram.at[gram_rows], gram_x.at[k], device) for k, (_, device) in enumerate(along_x)],
        gram_x,
    )
    cap10_copies = gather_x(cap10_all, cap10_copies)
    x_sum(q2, q2_x, q2_copies)
    q2_copies = z_step(q2, q2_z)
    core_sum(q1, q1_c, q1_copies)
    q1_copies = x_step(q1, q1_x)
    core_sum(q0, q0_c, q0_copies)
    q0_copies = x_step(q0, q0_x)

    cross_all[rows, :] = z_sum(cross, cross_z, cross_copies)
    cross_copies = gather_z(cross_all)
    arrived(gram_copies)
    gram_all[gram_rows, :] = total + (gram_x[0] + gram_x[1] + gram_x[2])
    piece = gram_all.at[gram_rows]
    gram_copies = group(
        [(piece, piece, device) for _, device in along_z], gram_all.at[pl.ds(0, 112)]
    )
    cap2_copies = gather_core(cap2_all, cap2_copies)
    q2_y[y % 2] = z_sum(q2, q2_z, q2_copies)
    q2_copies = exchange_y(q2_y, y % 2, 1)
    arrived(cap10_copies)
    cap10_copies = group(
        [
            (cap10_all.at[half_rows, 0:128], cap10_y.at[half_rows, 0:128], along_y[1]),
            (cap10_all.at[half_rows, 128:256], cap10_y.at[half_rows, 128:256], along_y[2]),
        ],
        cap10_y.at[half_rows],
    )
    x_sum(q1, q1_x, q1_copies)
    q1_copies = z_step(q1, q1_z)

    arrived(cap2_copies)
    pieces = jnp.concatenate(split(cap2_all[...]), axis=1)
    halves = [
        pick(256, lambda i: slot_row(i // 4) + i % 4 + 4 * h, pieces) for h in range(2)
    ]
    cap2 = tuple(
        jnp.concatenate([h[:, k : k + 256] for h in halves], axis=1) for k in (0, 256)
    )
    cross_copies = gather_x(cross_all, cross_copies)
    x_sum(q0, q0_x, q0_copies)
    q0_copies = z_step(q0, q0_z)
    arrived(q2_copies)
    c2 = few_rows_dot(jnp.concatenate([q2_y[1], q2_y[0]], axis=1), cap2, ((1,), (1,)))
    c2_all[rows, :] = c2
    arrived(gram_copies)
    piece = gram_all.at[gram_half]
    gram_copies = group([(piece, piece, core)], piece)
    arrived(cap10_copies)
    cap10_copies = group(
        [(b.at[half_rows], b.at[half_rows], core) for b in (cap10_all, cap10_y)], cap10_all
    )
    q1_own = z_sum(q1, q1_z, q1_copies)
    arrived(gram_copies)
    q1_y[y % 4] = q1_own - few_rows_dot(c2, split(gram_all[...]))
    q1_copies = exchange_y(q1_y, y % 4, 3)
    c2_copies = gather_z(c2_all)
    cross_copies = gather_core(cross_all, cross_copies)

    arrived(cap10_copies)
    even, even_pair = y % 2 == 0, (y // 2) % 2 == 0
    mine, theirs = cap10_all[:, 0:128], cap10_y[:, 0:128]
    cap1 = paired_rows(
        lambda i: slot_row(i // 2) + 4 * (i % 2),
        jnp.where(even, mine, theirs),
        jnp.where(even, theirs, mine),
    )
    arrived(cross_copies)
    cross_high, cross_low = split(cross_all[...])
    q0_own = z_sum(q0, q0_z, q0_copies)
    q0_own = q0_own - few_rows_dot(c2, (cross_high[0:256], cross_low[0:256]))

    arrived(q1_copies)
    c1 = few_rows_dot(
        jnp.concatenate([q1_y[2] + q1_y[3], q1_y[0] + q1_y[1]], axis=1), cap1, ((1,), (1,))
    )
    c1_all[rows, :] = c1
    q0_y[y] = q0_own - few_rows_dot(c1, (cross_high[256:512], cross_low[256:512]))
    q0_copies = exchange_y(q0_y, y, 7)
    c1_copies = gather_z(c1_all)
    c2_copies = gather_x(c2_all, c2_copies)
    mine, theirs = cap10_all[:, 128:256], cap10_y[:, 128:256]
    cap0 = paired_rows(
        lambda i: slot_row(i % 64) + 4 * (i // 64),
        jnp.where(even_pair, mine, theirs),
        jnp.where(even_pair, theirs, mine),
    )
    c2_copies = gather_core(c2_all, c2_copies)

    arrived(q0_copies)
    c0 = few_rows_dot(
        jnp.concatenate(
            [(q0_y[4] + q0_y[5]) + (q0_y[6] + q0_y[7]), (q0_y[0] + q0_y[1]) + (q0_y[2] + q0_y[3])],
            axis=1,
        ),
        cap0,
        ((1,), (1,)),
    )
    c0_all[rows, :] = c0
    c0_copies = gather_z(c0_all)
    c1_copies = gather_x(c1_all, c1_copies)
    arrived(c2_copies)
    out_ref[...] = x_ref[...] - dot(split(w2_ref[...]), split(c2_all[...]), ((1,), (1,)))
    c0_copies = gather_x(c0_all, c0_copies)
    c1_copies = gather_core(c1_all, c1_copies)
    arrived(c1_copies)
    out_ref[...] -= dot(split(w1_ref[...]), split(c1_all[...]), ((1,), (1,)))
    loads["w0"].wait()
    w0 = split(w0_ref[...])
    c0_copies = gather_core(c0_all, c0_copies)
    out_ref[:, half_rows] -= dot(w0, split(c0_all[half_rows, :]), ((1,), (1,)))
    arrived(c0_copies)
    half_rows = pl.ds(other_half, 256)
    out_ref[:, half_rows] -= dot(w0, split(c0_all[half_rows, :]), ((1,), (1,)))
    left()


def shards(
    rhs, v_basis0, w_basis0, cap_inv0, v_basis1, w_basis1, cap_inv1, v_basis2, w_basis2, cap_inv2
):
    groups = 40

    def f32(*shape):
        return pltpu.VMEM(shape, F32)

    return pl.pallas_call(
        kernel,
        out_shape=jax.ShapeDtypeStruct(rhs.shape, F32),
        in_specs=[pl.BlockSpec(memory_space=pltpu.HBM)] * 10,
        out_specs=pl.BlockSpec(memory_space=pltpu.VMEM),
        scratch_shapes=[
            f32(256, 512), f32(256, 256), f32(256, 256), f32(1, 512), f32(256, 256),
            f32(256, 256), f32(2, 512), f32(256, 256), f32(256, 256), f32(4, 512),
            pltpu.SemaphoreType.DMA((10,)),
            f32(256, 256), f32(128, 256), f32(7, 16, 256), f32(3, 16, 256), f32(256, 256),
            *[f32(512, 256)] * 4, *[f32(256, 256)] * 4, *[f32(3, 64, 256)] * 4, *[f32(7, 8, 256)] * 4,
            f32(512, 256), f32(512, 256), f32(512, 256), f32(512, 256),
            f32(512, 256), f32(512, 256), f32(512, 256),
            f32(2, 1, 512), f32(2, 8, 256), f32(4, 8, 256), f32(8, 8, 256),
            f32(1024, 256),
            pltpu.SemaphoreType.DMA((9,)),
            pltpu.SemaphoreType.DMA((groups,)),
        ],
        compiler_params=pltpu.CompilerParams(
            collective_id=0, has_side_effects=True, vmem_limit_bytes=52000 * 1024
        ),
    )(
        *(
            pltpu.with_memory_space_constraint(argument, pltpu.HBM)
            for argument in (
                rhs, v_basis0, w_basis0, cap_inv0, v_basis1, w_basis1, cap_inv1,
                v_basis2, w_basis2, cap_inv2,
            )
        )
    )


def solution(mesh):
    rows = P("rows", None)
    return jax.shard_map(
        shards, mesh=mesh, in_specs=(rows,) * 10, out_specs=rows, check_vma=False
    )
```
